32 devices in a mesh: dom: 2 (over y), row: 4 (over z), nbr: 4 (over x, core).
Axes of the slice: x: 2, y: 2, z: 4, core: 2. Of those that a mesh axis runs over, the one named last changes fastest.
Arguments:
- blocks: float32 [24, 12, 128, 128], P(('dom', 'row'), 'nbr'), parts along dimension 0, may hold values from -0.15625 to 0.15625
- partner_ids: int32 [24, 12], P(('dom', 'row'), 'nbr'), parts along dimension 0, may hold values from 0 to 11, as said below
- counts: int32 [24], P(('dom', 'row')), parts along dimension 0, may hold values from 1 to 12, as said below
- start: float32 [3072, 32], P(('dom', 'row')), parts along dimension 0, may hold values from -6 to 6
Outputs:
- basis: float32 [3072, 32], P(('dom', 'row')), parts along dimension 0
- ritz: float32 [64, 32], P('dom'), parts along dimension 0
The draws below stay inside these ranges and needn't reach their ends.
There are 2 independent parts, one for each index of `dom`. The reference program is written for one: setup_inputs(seed, part) draws one part's arguments, and reference() takes and returns one part's arrays. A program takes and returns all parts, laid end to end along the dimension named above; each array names one. Nothing has to cross between parts.
Inputs may be any that keep to these rules, and one draw needn't show every extreme that they name: partner_ids[i,0] == i; slots 1 to counts[i] - 1 hold distinct block columns greater than i; slots from counts[i] on hold i. counts[i] <= min(12, 12 - i); counts[0] == 12.
All inputs are finite; a program needn't handle non-finite values.
Results may differ from the reference program's by a relative error of at most 0.0001.
Values sent between devices are 32-bit elements; how exact they have to be, the bound alone decides.
A program may use at most 64 MiB of HBM per device.

```python
import jax
import jax.numpy as jnp
from jax import lax

BS = 128
K = 32
ITERS = 2
NBLK = 12
SLOTS = 12
NROWS = 1536


def pattern(key):
    base = jax.random.fold_in(key, 7)
    count_key = jax.random.fold_in(base, 1)
    pick_key = jax.random.fold_in(base, 2)
    row_index = jnp.arange(NBLK, dtype=jnp.int32)
    room = jnp.minimum(SLOTS, NBLK - row_index)
    wanted = jax.random.randint(count_key, (NBLK,), 1, SLOTS + 1, dtype=jnp.int32)
    counts = jnp.where(row_index == 0, SLOTS, jnp.minimum(wanted, room)).astype(jnp.int32)
    scores = jax.random.randint(pick_key, (NBLK, NBLK), 0, 2 ** 20, dtype=jnp.int32)
    column = row_index[None, :]
    ranked = jnp.where(column > row_index[:, None], scores * NBLK + column, -1 - column)
    ranked_values, picks = lax.top_k(ranked, SLOTS - 1)
    partners = jnp.concatenate([row_index[:, None], picks.astype(jnp.int32)], axis=1)
    slot_index = jnp.arange(SLOTS, dtype=jnp.int32)
    partners = jnp.where(slot_index[None, :] < counts[:, None], partners, row_index[:, None])
    return (partners.astype(jnp.int32), counts)


def draw_partner_ids(key, part):
    return pattern(key)[0]


def draw_counts(key, part):
    return pattern(key)[1]


def level_of(rng, extent, pieces, low, top_value):
    gain = 1.0
    for position, parts in pieces:
        steps = jax.random.uniform(jax.random.fold_in(jax.random.fold_in(rng, 6), position), (parts,), jnp.float32, low / len(pieces), top_value / len(pieces))
        gain = gain * jnp.repeat(jnp.exp(steps), extent[position] // parts).reshape((-1,) + (1,) * (len(extent) - 1 - position))
    return gain


def centred(stream_key, dims, deviation, most, split=(), kind=jnp.bfloat16):
    values = jax.random.normal(stream_key, dims, jnp.float32) * deviation
    if len(split) > 0:
        values = level_of(stream_key, dims, split, -0.22, 0.18) * values
    return jnp.clip(values, min=-most, max=most).astype(kind)


def setup_inputs(seed: int = 0, part: int = 0) -> dict:
    splits = jax.random.split(jax.random.key(seed), 5)
    own_keys = jax.random.split(jax.random.fold_in(splits[4], part), 5)
    return {
        "blocks": centred(own_keys[0], (NBLK, SLOTS, BS, BS), (SLOTS * BS) ** -0.5, 0.15625, ((0, 4), (1, 4)), jnp.float32),
        "partner_ids": draw_partner_ids(jax.random.fold_in(jax.random.fold_in(splits[4], part), 71), part),
        "counts": draw_counts(jax.random.fold_in(jax.random.fold_in(splits[4], part), 71), part),
        "start": centred(own_keys[3], (NROWS, K), 1.0, 6.0, ((0, 4),), jnp.float32),
    }


HIGH = lax.Precision.HIGHEST

def apply_matrix(blocks, partner_ids, counts, basis):
    tiles = basis.reshape(NBLK, BS, K)
    slot_index = jnp.arange(SLOTS, dtype=jnp.int32)
    row_index = jnp.arange(NBLK, dtype=jnp.int32)
    valid = slot_index[None, :] < counts[:, None]
    weight = jnp.where(valid, jnp.where(partner_ids == row_index[:, None], 0.5, 1.0), 0.0).astype(jnp.float32)

    def per_row(packed):
        tile_block, ids_row, weight_row, own_tile = packed
        far = tiles[ids_row] * weight_row[:, None, None]
        direct = jnp.einsum('pab,pbk->ak', tile_block, far, precision=HIGH)
        transposed = jnp.einsum('pab,ak->pbk', tile_block, own_tile, precision=HIGH) * weight_row[:, None, None]
        return (direct, transposed)
    direct, transposed = lax.map(per_row, (blocks, partner_ids, weight, tiles))
    spread = jax.ops.segment_sum(transposed.reshape(NBLK * SLOTS, BS, K), partner_ids.reshape(-1), num_segments=NBLK)
    return (direct + spread).reshape(NROWS, K)

def reference(blocks, partner_ids, counts, start):
    prior = start
    cross = jnp.zeros((K, K), jnp.float32)
    for step in range(ITERS):
        image = apply_matrix(blocks, partner_ids, counts, prior)
        gram = jnp.dot(image.T, image, precision=HIGH) / NROWS
        cross = jnp.dot(prior.T, image, precision=HIGH) / NROWS
        lower = jnp.linalg.cholesky(gram)
        prior = lax.linalg.triangular_solve(lower, image, left_side=False, lower=True, transpose_a=True)
    return (prior, cross)
```

```python
import functools

import jax
import jax.numpy as jnp
from jax import lax
from jax.experimental import pallas as pl
from jax.experimental.pallas import tpu as pltpu
from jax.sharding import PartitionSpec as P

ITERS = 2
DIRECT_PEERS = 16

HIGH = lax.Precision.HIGHEST
F32 = jnp.float32
BF16 = jnp.bfloat16


def orthonormal(image, gram, total):
    lower = jnp.linalg.cholesky(gram / total)
    return lax.linalg.triangular_solve(lower, image, left_side=False, lower=True, transpose_a=True)


def body(blocks, partner_ids, counts, start):
    block_rows, slots_here = partner_ids.shape
    block_size = blocks.shape[2]
    columns = start.shape[1]
    row_count = lax.axis_size("row")
    all_blocks = block_rows * row_count
    total = all_blocks * block_size
    first_row = lax.axis_index("row") * block_rows
    rows_here = first_row + jnp.arange(block_rows, dtype=jnp.int32)
    slot_index = lax.axis_index("nbr") * slots_here + jnp.arange(slots_here, dtype=jnp.int32)
    valid = slot_index[None, :] < counts[:, None]
    weight = jnp.where(valid, jnp.where(partner_ids == rows_here[:, None], 0.5, 1.0), 0.0).astype(
        jnp.float32
    )
    targets = jnp.concatenate([partner_ids.reshape(-1), rows_here])
    whole = lax.all_gather(start, "row", axis=0, tiled=True)
    cross = jnp.zeros((columns, columns), jnp.float32)
    prior = start
    for step in range(ITERS):
        tiles = whole.reshape(all_blocks, block_size, columns)
        far = tiles[partner_ids] * weight[:, :, None, None]
        near = lax.dynamic_slice_in_dim(tiles, first_row, block_rows, 0)
        direct = jnp.einsum("ipab,ipbk->iak", blocks, far, precision=HIGH)
        transposed = (
            jnp.einsum("ipab,iak->ipbk", blocks, near, precision=HIGH) * weight[:, :, None, None]
        )
        items = jnp.concatenate(
            [transposed.reshape(block_rows * slots_here, block_size, columns), direct], axis=0
        )
        placed = jnp.zeros((all_blocks, block_size, columns), jnp.float32).at[targets].add(items)
        summed = lax.psum_scatter(
            placed.reshape(total, columns), "row", scatter_dimension=0, tiled=True
        )
        image = lax.psum(summed, "nbr")
        gram, cross = lax.psum(
            (jnp.dot(image.T, image, precision=HIGH), jnp.dot(prior.T, image, precision=HIGH)),
            "row",
        )
        cross = cross / total
        prior = orthonormal(image, gram, total)
        if step + 1 < ITERS:
            whole = lax.all_gather(prior, "row", axis=0, tiled=True)
    return (prior, cross)


def split(x):
    high = x.astype(BF16)
    return high, (x - high.astype(F32)).astype(BF16)


def dot_nt(a, b):
    return lax.dot_general(a, b, (((1,), (1,)), ((), ())), precision=HIGH, preferred_element_type=F32)


def dot_nn(a, b, precision=HIGH):
    return lax.dot_general(
        a, b, (((1,), (0,)), ((), ())), precision=precision, preferred_element_type=F32
    )


def inverse_factor(gram_at, columns, lanes):
    row = lax.broadcasted_iota(jnp.int32, (columns, lanes), 0)
    lane = lax.broadcasted_iota(jnp.int32, (columns, lanes), 1)
    work = jnp.where(lane < columns, jnp.where(lane == row, 1.0, 0.0), gram_at)
    work = jnp.where(lane < 2 * columns, work, 0.0)
    for k in range(columns):
        pivot = work[k : k + 1, :]
        at = columns + k
        inverse = 1.0 / pivot[:, at : at + 1]
        factor = jnp.where(row[:, :1] > k, work[:, at : at + 1] * inverse, 0.0)
        work = work - factor * pivot
    diagonal = jnp.sum(jnp.where(lane == row + columns, work, 0.0), axis=1, keepdims=True)
    return (work * (1.0 / jnp.sqrt(diagonal)))[:, :columns]


def kernel(
    rows, nbrs, ids_ref, counts_ref, start_ref, blocks_ref, basis_ref, ritz_ref,
    held, straight, turned, sel, weight, whole, part, inbox, stats, stats_in, images,
    blocks_sem, start_send, start_recv, rs_send, rs_recv, ag_send, ag_recv,
    st_send, st_recv, im_send, im_recv,
):
    block_rows, slots = ids_ref.shape
    columns = start_ref.shape[0]
    size = blocks_ref.shape[2]
    tiles = block_rows * rows
    total = tiles * size
    group = rows * nbrs
    my_row, my_nbr = lax.axis_index("row"), lax.axis_index("nbr")
    me = my_row * nbrs + my_nbr
    owner = my_nbr < block_rows
    my_tile = my_row * block_rows + lax.min(my_nbr, block_rows - 1)

    def place(d):
        peer = lax.rem(me + d, group)
        return peer // nbrs, lax.rem(peer, nbrs)

    def device(r, n):
        return {"row": r, "nbr": n}

    barrier = pltpu.get_barrier_semaphore()
    for d in range(1, group):
        r, n = place(d)
        pl.semaphore_signal(
            barrier, inc=1, device_id=device(r, n), device_id_type=pl.DeviceIdType.MESH
        )
    load = pltpu.make_async_copy(blocks_ref, held, blocks_sem)
    load.start()
    for i in range(block_rows):
        whole[0, my_row * block_rows + i] = start_ref[:, i * size : (i + 1) * size]
    for i in range(block_rows):
        for p in range(slots):
            j = ids_ref[i, p]
            valid = my_nbr * slots + p < counts_ref[i]
            c = jnp.where(valid, jnp.where(j == my_row * block_rows + i, 0.5, 1.0), 0.0)
            weight[i * slots + p] = c
            for t in range(tiles):
                sel[(i * slots + p) * tiles + t] = jnp.where(j == t, c, 0.0)
    pl.semaphore_wait(barrier, group - 1)

    def start_copy(d, i):
        r = lax.rem(my_row + d, rows)
        return pltpu.make_async_remote_copy(
            src_ref=start_ref.at[:, pl.ds(i * size, size)],
            dst_ref=whole.at[0, my_row * block_rows + i],
            send_sem=start_send.at[d - 1, i],
            recv_sem=start_recv.at[d - 1, i],
            device_id=device(r, my_nbr),
            device_id_type=pl.DeviceIdType.MESH,
        )

    for d in range(1, rows):
        for i in range(block_rows):
            start_copy(d, i).start()

    load.wait()
    span = slots * size
    for i in range(block_rows):
        for p in range(slots):
            block = held[i, p]
            high, low = split(block)
            straight[i, :size, p * size : (p + 1) * size] = high
            straight[i, size:, p * size : (p + 1) * size] = low
            high, low = split(block.T)
            turned[i, p * size : (p + 1) * size, :] = high
            turned[i, span + p * size : span + (p + 1) * size, :] = low

    for d in range(1, rows):
        for i in range(block_rows):
            start_copy(d, i).wait_recv()

    def apply(step):
        moved = []
        for i in range(block_rows):
            near = jnp.concatenate(split(whole[step, my_row * block_rows + i]), axis=0)
            out = dot_nn(jnp.concatenate([near, near], axis=1), straight[i], None)
            moved.append(out[:columns] + out[columns:])
        for t in range(tiles):
            summed = None
            for i in range(block_rows):
                for p in range(slots):
                    term = moved[i][:, p * size : (p + 1) * size] * sel[(i * slots + p) * tiles + t]
                    summed = term if summed is None else summed + term
            part[step, t] = summed
        for i in range(block_rows):
            far = []
            for p in range(slots):
                tile = whole[step, ids_ref[i, p]] * weight[i * slots + p]
                far.append(jnp.concatenate(split(tile), axis=0))
            out = dot_nn(jnp.concatenate(far + far, axis=1), turned[i], None)
            t = my_row * block_rows + i
            part[step, t] = part[step, t] + (out[:columns] + out[columns:])

    def sum_copy(step, d):
        r, n = place(d)
        return pltpu.make_async_remote_copy(
            src_ref=part.at[step, r * block_rows + lax.min(n, block_rows - 1)],
            dst_ref=inbox.at[step, d - 1],
            send_sem=rs_send.at[step, d - 1],
            recv_sem=rs_recv.at[step, d - 1],
            device_id=device(r, n),
            device_id_type=pl.DeviceIdType.MESH,
        )

    def send_sums(step):
        for d in range(1, group):
            @pl.when(place(d)[1] < block_rows)
            def _():
                sum_copy(step, d).start()

    def gather_sums(step):
        summed = part[step, my_tile]
        for d in range(1, group):
            sum_copy(step, d).wait_recv()
            summed = summed + inbox[step, d - 1]
        return summed

    def image_copy(d):
        r, n = place(d)
        return pltpu.make_async_remote_copy(
            src_ref=whole.at[1, my_tile],
            dst_ref=whole.at[1, my_tile],
            send_sem=ag_send.at[d - 1],
            recv_sem=ag_recv.at[d - 1],
            device_id=device(r, n),
            device_id_type=pl.DeviceIdType.MESH,
        )

    def from_owner(d):
        return lax.rem(me + group - d, nbrs) < block_rows

    apply(0)
    send_sums(0)

    @pl.when(owner)
    def _():
        whole[1, my_tile] = gather_sums(0)
        for d in range(1, group):
            image_copy(d).start()

    for d in range(1, group):
        @pl.when(from_owner(d))
        def _():
            image_copy(d).wait_recv()

    apply(1)
    send_sums(1)

    gram = jnp.zeros((columns, size), F32)
    blank = jnp.zeros((columns, size), F32)
    for t in range(tiles):
        tile = whole[1, t]
        gram = gram + dot_nt(tile, jnp.concatenate([blank, tile, blank, blank], axis=0))
    first = inverse_factor(gram / total, columns, size)

    def stats_copy(d):
        r, n = place(d)
        return pltpu.make_async_remote_copy(
            src_ref=stats,
            dst_ref=stats_in.at[d - 1],
            send_sem=st_send.at[d - 1],
            recv_sem=st_recv.at[d - 1],
            device_id=device(r, n),
            device_id_type=pl.DeviceIdType.MESH,
        )

    def own_copy(d):
        return pltpu.make_async_remote_copy(
            src_ref=images.at[lax.min(my_nbr, block_rows - 1)],
            dst_ref=images.at[lax.min(my_nbr, block_rows - 1)],
            send_sem=im_send.at[d - 1],
            recv_sem=im_recv.at[d - 1],
            device_id=device(my_row, lax.rem(my_nbr + d, nbrs)),
            device_id_type=pl.DeviceIdType.MESH,
        )

    def own_from(d):
        return lax.rem(my_nbr + nbrs - d, nbrs) < block_rows

    half = columns // 2

    @pl.when(owner)
    def _():
        prior = dot_nn(first, whole[1, my_tile])
        image = dot_nn(first, gather_sums(1))
        images[my_nbr] = image
        both = dot_nt(image, jnp.concatenate([image, blank, blank, blank], axis=0))
        other = dot_nt(prior, jnp.concatenate([blank, image, blank, blank], axis=0))
        both = both + other
        stats[...] = both[:half] + pltpu.roll(both[half:], 2 * columns, 1)
        for d in range(1, group):
            stats_copy(d).start()
        for d in range(1, nbrs):
            own_copy(d).start()

    @pl.when(jnp.logical_not(owner))
    def _():
        stats[...] = jnp.zeros_like(stats)

    stats_in[group - 1] = stats[...]
    for d in range(1, group):
        @pl.when(from_owner(d))
        def _():
            stats_copy(d).wait_recv()

        @pl.when(jnp.logical_not(from_owner(d)))
        def _():
            stats_in[d - 1] = jnp.zeros_like(stats)

    packed = stats_in[group - 1]
    for d in range(1, group):
        packed = packed + stats_in[d - 1]
    packed = packed / total
    rest = jnp.concatenate([packed, pltpu.roll(packed, 2 * columns, 1)], axis=0)
    last = inverse_factor(pltpu.roll(rest, columns, 1), columns, size)
    ritz_ref[...] = pltpu.roll(rest, size - columns, 1)[:, :columns]
    for d in range(1, nbrs):
        @pl.when(own_from(d))
        def _():
            own_copy(d).wait_recv()
    for i in range(block_rows):
        basis_ref[:, i * size : (i + 1) * size] = dot_nn(last, images[i])

    for d in range(1, rows):
        for i in range(block_rows):
            start_copy(d, i).wait_send()
    for step in range(ITERS):
        for d in range(1, group):
            @pl.when(place(d)[1] < block_rows)
            def _():
                sum_copy(step, d).wait_send()

    @pl.when(owner)
    def _():
        for d in range(1, group):
            image_copy(d).wait_send()
            stats_copy(d).wait_send()
        for d in range(1, nbrs):
            own_copy(d).wait_send()


def direct_body(rows, nbrs, blocks, partner_ids, counts, start):
    block_rows, slots = partner_ids.shape
    size = blocks.shape[2]
    columns = start.shape[1]
    tiles = block_rows * rows
    group = rows * nbrs
    dma = pltpu.SemaphoreType.DMA
    basis, ritz = pl.pallas_call(
        functools.partial(kernel, rows, nbrs),
        out_shape=(
            jax.ShapeDtypeStruct((columns, block_rows * size), F32),
            jax.ShapeDtypeStruct((columns, columns), F32),
        ),
        in_specs=[
            pl.BlockSpec(memory_space=pltpu.SMEM),
            pl.BlockSpec(memory_space=pltpu.SMEM),
            pl.BlockSpec(memory_space=pltpu.VMEM),
            pl.BlockSpec(memory_space=pl.ANY),
        ],
        out_specs=(
            pl.BlockSpec(memory_space=pltpu.VMEM),
            pl.BlockSpec(memory_space=pltpu.VMEM),
        ),
        scratch_shapes=[
            pltpu.VMEM((block_rows, slots, size, size), F32),
            pltpu.VMEM((block_rows, 2 * size, slots * size), BF16),
            pltpu.VMEM((block_rows, 2 * slots * size, size), BF16),
            pltpu.SMEM((block_rows * slots * tiles,), F32),
            pltpu.SMEM((block_rows * slots,), F32),
            pltpu.VMEM((2, tiles, columns, size), F32),
            pltpu.VMEM((2, tiles, columns, size), F32),
            pltpu.VMEM((2, group - 1, columns, size), F32),
            pltpu.VMEM((columns // 2, size), F32),
            pltpu.VMEM((group, columns // 2, size), F32),
            pltpu.VMEM((block_rows, columns, size), F32),
            dma,
            dma((rows - 1, block_rows)),
            dma((rows - 1, block_rows)),
            dma((2, group - 1)),
            dma((2, group - 1)),
            dma((group - 1,)),
            dma((group - 1,)),
            dma((group - 1,)),
            dma((group - 1,)),
            dma((nbrs - 1,)),
            dma((nbrs - 1,)),
        ],
        compiler_params=pltpu.CompilerParams(collective_id=0, has_side_effects=True),
    )(partner_ids, counts, start.T, blocks)
    return basis.T, ritz


def solution(mesh):
    rows, nbrs = mesh.shape["row"], mesh.shape["nbr"]

    def program(blocks, partner_ids, counts, start):
        block_rows = partner_ids.shape[0]
        size, columns = blocks.shape[2], start.shape[1]
        if rows * nbrs <= DIRECT_PEERS and block_rows <= nbrs and size == 128 and 4 * columns == size:
            return direct_body(rows, nbrs, blocks, partner_ids, counts, start)
        return body(blocks, partner_ids, counts, start)

    return jax.shard_map(
        program,
        mesh=mesh,
        in_specs=(
            P(("dom", "row"), "nbr", None, None),
            P(("dom", "row"), "nbr"),
            P(("dom", "row")),
            P(("dom", "row"), None),
        ),
        out_specs=(P(("dom", "row"), None), P("dom", None)),
        check_vma=False,
    )
```

```python
import functools

import jax
import jax.numpy as jnp
from jax import lax
from jax.experimental import pallas as pl
from jax.experimental.pallas import tpu as pltpu
from jax.sharding import PartitionSpec as P

ITERS = 2
DIRECT_PEERS = 16

HIGH = lax.Precision.HIGHEST
F32 = jnp.float32
BF16 = jnp.bfloat16


def orthonormal(image, gram, total):
    lower = jnp.linalg.cholesky(gram / total)
    return lax.linalg.triangular_solve(lower, image, left_side=False, lower=True, transpose_a=True)


def body(blocks, partner_ids, counts, start):
    block_rows, slots_here = partner_ids.shape
    block_size = blocks.shape[2]
    columns = start.shape[1]
    row_count = lax.axis_size("row")
    all_blocks = block_rows * row_count
    total = all_blocks * block_size
    first_row = lax.axis_index("row") * block_rows
    rows_here = first_row + jnp.arange(block_rows, dtype=jnp.int32)
    slot_index = lax.axis_index("nbr") * slots_here + jnp.arange(slots_here, dtype=jnp.int32)
    valid = slot_index[None, :] < counts[:, None]
    weight = jnp.where(valid, jnp.where(partner_ids == rows_here[:, None], 0.5, 1.0), 0.0).astype(
        jnp.float32
    )
    targets = jnp.concatenate([partner_ids.reshape(-1), rows_here])
    whole = lax.all_gather(start, "row", axis=0, tiled=True)
    cross = jnp.zeros((columns, columns), jnp.float32)
    prior = start
    for step in range(ITERS):
        tiles = whole.reshape(all_blocks, block_size, columns)
        far = tiles[partner_ids] * weight[:, :, None, None]
        near = lax.dynamic_slice_in_dim(tiles, first_row, block_rows, 0)
        direct = jnp.einsum("ipab,ipbk->iak", blocks, far, precision=HIGH)
        transposed = (
            jnp.einsum("ipab,iak->ipbk", blocks, near, precision=HIGH) * weight[:, :, None, None]
        )
        items = jnp.concatenate(
            [transposed.reshape(block_rows * slots_here, block_size, columns), direct], axis=0
        )
        placed = jnp.zeros((all_blocks, block_size, columns), jnp.float32).at[targets].add(items)
        summed = lax.psum_scatter(
            placed.reshape(total, columns), "row", scatter_dimension=0, tiled=True
        )
        image = lax.psum(summed, "nbr")
        gram, cross = lax.psum(
            (jnp.dot(image.T, image, precision=HIGH), jnp.dot(prior.T, image, precision=HIGH)),
            "row",
        )
        cross = cross / total
        prior = orthonormal(image, gram, total)
        if step + 1 < ITERS:
            whole = lax.all_gather(prior, "row", axis=0, tiled=True)
    return (prior, cross)


def split(x):
    high = x.astype(BF16)
    return high, (x - high.astype(F32)).astype(BF16)


def dot_nt(a, b):
    return lax.dot_general(a, b, (((1,), (1,)), ((), ())), precision=HIGH, preferred_element_type=F32)


def dot_nn(a, b, precision=HIGH):
    return lax.dot_general(
        a, b, (((1,), (0,)), ((), ())), precision=precision, preferred_element_type=F32
    )


def inverse_factor(gram_at, columns, lanes):
    row = lax.broadcasted_iota(jnp.int32, (columns, lanes), 0)
    lane = lax.broadcasted_iota(jnp.int32, (columns, lanes), 1)
    work = jnp.where(lane < columns, jnp.where(lane == row, 1.0, 0.0), gram_at)
    work = jnp.where(lane < 2 * columns, work, 0.0)
    for k in range(columns):
        pivot = work[k : k + 1, :]
        at = columns + k
        inverse = 1.0 / pivot[:, at : at + 1]
        factor = jnp.where(row[:, :1] > k, work[:, at : at + 1] * inverse, 0.0)
        work = work - factor * pivot
    diagonal = jnp.sum(jnp.where(lane == row + columns, work, 0.0), axis=1, keepdims=True)
    return (work * (1.0 / jnp.sqrt(diagonal)))[:, :columns]


def kernel(
    rows, nbrs, ids_ref, counts_ref, start_ref, blocks_ref, basis_ref, ritz_ref,
    held, straight, turned, sel, weight, begun, first_image, part, inbox, near_part, near_inbox, total_sum,
    grams, stats, images,
    blocks_sem, start_send, start_recv, rs_send, rs_recv, near_send, near_recv, ag_send, ag_recv,
    gram_send, gram_recv, st_send, st_recv, im_send, im_recv,
):
    block_rows, slots = ids_ref.shape
    columns = start_ref.shape[0]
    size = blocks_ref.shape[2]
    tiles = block_rows * rows
    total = tiles * size
    group = rows * nbrs
    my_row, my_nbr = lax.axis_index("row"), lax.axis_index("nbr")
    me = my_row * nbrs + my_nbr
    owner = my_nbr < block_rows
    my_slot = lax.min(my_nbr, block_rows - 1)
    first_tile = my_row * block_rows
    my_tile = first_tile + my_slot
    whole = (begun, first_image)
    blank = jnp.zeros((columns, size), F32)

    def send(src, dst, send_sem, recv_sem, r, n):
        return pltpu.make_async_remote_copy(
            src_ref=src, dst_ref=dst, send_sem=send_sem, recv_sem=recv_sem,
            device_id={"row": r, "nbr": n}, device_id_type=pl.DeviceIdType.MESH,
        )

    barrier = pltpu.get_barrier_semaphore()
    for d in range(1, group):
        peer = lax.rem(me + d, group)
        pl.semaphore_signal(
            barrier, inc=1, device_id={"row": peer // nbrs, "nbr": lax.rem(peer, nbrs)},
            device_id_type=pl.DeviceIdType.MESH,
        )
    load = pltpu.make_async_copy(blocks_ref, held, blocks_sem)
    load.start()
    for i in range(block_rows):
        begun[first_tile + i] = start_ref[:, i * size : (i + 1) * size]
    for q in range(rows - 1):
        @pl.when(q < my_row)
        def _():
            for i in range(block_rows):
                begun[q * block_rows + i] = blank
                first_image[q * block_rows + i] = blank
    for i in range(block_rows):
        for p in range(slots):
            j = ids_ref[i, p]
            valid = my_nbr * slots + p < counts_ref[i]
            c = jnp.where(valid, jnp.where(j == first_tile + i, 0.5, 1.0), 0.0)
            weight[i * slots + p] = c
            for t in range(tiles):
                sel[(i * slots + p) * tiles + t] = jnp.where(j == t, c, 0.0)

    load.wait()
    span = slots * size
    for i in range(block_rows):
        for p in range(slots):
            block = held[i, p]
            high, low = split(block)
            straight[i, :size, p * size : (p + 1) * size] = high
            straight[i, size:, p * size : (p + 1) * size] = low
            high, low = split(block.T)
            turned[i, p * size : (p + 1) * size, :] = high
            turned[i, span + p * size : span + (p + 1) * size, :] = low

    def transposed(step):
        moved = []
        for i in range(block_rows):
            near = jnp.concatenate(split(whole[step][first_tile + i]), axis=0)
            out = dot_nn(jnp.concatenate([near, near], axis=1), straight[i], None)
            moved.append(out[:columns] + out[columns:])
        for t in range(tiles):
            summed = None
            for i in range(block_rows):
                for p in range(slots):
                    term = moved[i][:, p * size : (p + 1) * size] * sel[(i * slots + p) * tiles + t]
                    summed = term if summed is None else summed + term
            part[step, t] = summed

    def direct(step):
        for i in range(block_rows):
            far = []
            for p in range(slots):
                tile = whole[step][ids_ref[i, p]] * weight[i * slots + p]
                far.append(jnp.concatenate(split(tile), axis=0))
            out = dot_nn(jnp.concatenate(far + far, axis=1), turned[i], None)
            near_part[step, i] = out[:columns] + out[columns:]

    def start_copy(q, i):
        return send(
            start_ref.at[:, pl.ds(i * size, size)], begun.at[first_tile + i],
            start_send.at[q, i], start_recv.at[my_row, i], q, my_nbr,
        )

    def start_wait(q, i):
        send(
            start_ref.at[:, pl.ds(i * size, size)], begun.at[q * block_rows + i],
            start_send.at[q, i], start_recv.at[q, i], q, my_nbr,
        ).wait_recv()

    def sum_copy(step, r, n):
        return send(
            part.at[step, r * block_rows + n], inbox.at[step, me],
            rs_send.at[step, r, n], rs_recv.at[step, me], r, n,
        )

    def sum_wait(step, r, n):
        send(
            part.at[step, my_tile], inbox.at[step, r * nbrs + n],
            rs_send.at[step, 0, 0], rs_recv.at[step, r * nbrs + n], r, n,
        ).wait_recv()

    def each_sum(step, act):
        for r in range(rows):
            for n in range(block_rows):
                @pl.when(jnp.logical_and(r >= my_row, r * nbrs + n != me))
                def _():
                    act(sum_copy(step, r, n))

    def near_copy(step, i):
        return send(
            near_part.at[step, i], near_inbox.at[step, my_nbr],
            near_send.at[step, i], near_recv.at[step, my_nbr], my_row, i,
        )

    def near_wait(step, n):
        send(
            near_part.at[step, my_slot], near_inbox.at[step, n],
            near_send.at[step, 0], near_recv.at[step, n], my_row, n,
        ).wait_recv()

    def each_near(step, act):
        for i in range(block_rows):
            @pl.when(i != my_nbr)
            def _():
                act(near_copy(step, i))

    def gather_sums(step):
        total_sum[...] = part[step, my_tile] + near_part[step, my_slot]
        for q in range(rows - 1):
            @pl.when(q < my_row)
            def _():
                for n in range(nbrs):
                    sum_wait(step, q, n)
                summed = inbox[step, q * nbrs]
                for n in range(1, nbrs):
                    summed = summed + inbox[step, q * nbrs + n]
                total_sum[...] += summed
        for e in range(1, nbrs):
            n = lax.rem(my_nbr + e, nbrs)
            sum_wait(step, my_row, n)
            total_sum[...] += inbox[step, my_row * nbrs + n]
        for e in range(1, nbrs):
            n = lax.rem(my_nbr + e, nbrs)
            near_wait(step, n)
            total_sum[...] += near_inbox[step, n]
        return total_sum[...]

    def image_copy(r, n):
        return send(
            first_image.at[my_tile], first_image.at[my_tile],
            ag_send.at[r, n], ag_recv.at[my_tile], r, n,
        )

    def image_wait(t):
        send(
            first_image.at[t], first_image.at[t], ag_send.at[0, 0], ag_recv.at[t], my_row, my_nbr
        ).wait_recv()

    def near_images(act):
        for e in range(1, nbrs):
            act(image_copy(my_row, lax.rem(my_nbr + e, nbrs)))

    def far_images(act):
        for q in range(rows - 1):
            @pl.when(q < my_row)
            def _():
                for n in range(nbrs):
                    act(image_copy(q, n))

    def gram_copy(t):
        return send(
            grams.at[my_tile], grams.at[my_tile],
            gram_send.at[t], gram_recv.at[my_tile], t // block_rows, t % block_rows,
        )

    def gram_wait(t):
        send(
            grams.at[t], grams.at[t], gram_send.at[t], gram_recv.at[t],
            t // block_rows, t % block_rows,
        ).wait_recv()

    def each_gram(act):
        for t in range(tiles):
            @pl.when(t != my_tile)
            def _():
                act(t)

    def stats_copy(g):
        return send(
            stats.at[my_tile], stats.at[my_tile],
            st_send.at[g], st_recv.at[my_tile], g // nbrs, g % nbrs,
        )

    def stats_wait(t):
        send(
            stats.at[t], stats.at[t], st_send.at[0], st_recv.at[t], my_row, my_nbr
        ).wait_recv()

    def each_stats(act):
        for g in range(group):
            @pl.when(g != me)
            def _():
                act(stats_copy(g))

    def own_copy(e):
        return send(
            images.at[my_slot], images.at[my_slot],
            im_send.at[e - 1], im_recv.at[my_slot], my_row, lax.rem(my_nbr + e, nbrs),
        )

    def own_wait(i):
        send(
            images.at[i], images.at[i], im_send.at[0], im_recv.at[i], my_row, my_nbr
        ).wait_recv()

    def each_start(act):
        for q in range(rows - 1):
            @pl.when(q < my_row)
            def _():
                for i in range(block_rows):
                    act(start_copy(q, i))

    def begin(copy):
        copy.start()

    def end(copy):
        copy.wait_send()

    transposed(0)
    pl.semaphore_wait(barrier, group - 1)
    each_start(begin)
    each_sum(0, begin)
    for q in range(1, rows):
        @pl.when(q > my_row)
        def _():
            for i in range(block_rows):
                start_wait(q, i)
    direct(0)
    each_near(0, begin)

    quarter, half = columns // 4, columns // 2

    @pl.when(owner)
    def _():
        tile = gather_sums(0)
        first_image[my_tile] = tile
        near_images(begin)
        far_images(begin)
        gram = dot_nt(tile, jnp.concatenate([tile, blank, blank, blank], axis=0))
        packed = gram[:quarter]
        for g in range(1, 4):
            packed = packed + pltpu.roll(gram[g * quarter : (g + 1) * quarter], g * columns, 1)
        grams[my_tile] = packed
        each_gram(lambda t: gram_copy(t).start())

    for i in range(block_rows):
        @pl.when(i != my_nbr)
        def _():
            image_wait(first_tile + i)
    transposed(1)
    each_sum(1, begin)
    for q in range(1, rows):
        @pl.when(q > my_row)
        def _():
            for i in range(block_rows):
                image_wait(q * block_rows + i)
    direct(1)
    each_near(1, begin)

    @pl.when(owner)
    def _():
        each_gram(gram_wait)
        packed = grams[0]
        for t in range(1, tiles):
            packed = packed + grams[t]
        packed = packed / total
        gram = jnp.concatenate(
            [pltpu.roll(packed, size - g * columns, 1) if g else packed for g in range(4)], axis=0
        )
        first = inverse_factor(pltpu.roll(gram, columns, 1), columns, size)
        prior = dot_nn(first, first_image[my_tile])
        image = dot_nn(first, gather_sums(1))
        images[my_nbr] = image
        both = dot_nt(image, jnp.concatenate([image, blank, blank, blank], axis=0))
        other = dot_nt(prior, jnp.concatenate([blank, image, blank, blank], axis=0))
        both = both + other
        stats[my_tile] = both[:half] + pltpu.roll(both[half:], 2 * columns, 1)
        each_stats(begin)
        for e in range(1, nbrs):
            own_copy(e).start()

    for t in range(tiles):
        @pl.when(jnp.logical_or(jnp.logical_not(owner), t != my_tile))
        def _():
            stats_wait(t)
    packed = stats[0]
    for t in range(1, tiles):
        packed = packed + stats[t]
    packed = packed / total
    rest = jnp.concatenate([packed, pltpu.roll(packed, 2 * columns, 1)], axis=0)
    last = inverse_factor(pltpu.roll(rest, columns, 1), columns, size)
    ritz_ref[...] = pltpu.roll(rest, size - columns, 1)[:, :columns]
    for i in range(block_rows):
        @pl.when(i != my_nbr)
        def _():
            own_wait(i)
    for i in range(block_rows):
        basis_ref[:, i * size : (i + 1) * size] = dot_nn(last, images[i])

    each_start(end)
    for step in range(ITERS):
        each_sum(step, end)
        each_near(step, end)

    @pl.when(owner)
    def _():
        near_images(end)
        far_images(end)
        each_gram(lambda t: gram_copy(t).wait_send())
        each_stats(end)
        for e in range(1, nbrs):
            own_copy(e).wait_send()


def direct_body(rows, nbrs, blocks, partner_ids, counts, start):
    block_rows, slots = partner_ids.shape
    size = blocks.shape[2]
    columns = start.shape[1]
    tiles = block_rows * rows
    group = rows * nbrs
    dma = pltpu.SemaphoreType.DMA
    basis, ritz = pl.pallas_call(
        functools.partial(kernel, rows, nbrs),
        out_shape=(
            jax.ShapeDtypeStruct((columns, block_rows * size), F32),
            jax.ShapeDtypeStruct((columns, columns), F32),
        ),
        in_specs=[
            pl.BlockSpec(memory_space=pltpu.SMEM),
            pl.BlockSpec(memory_space=pltpu.SMEM),
            pl.BlockSpec(memory_space=pltpu.VMEM),
            pl.BlockSpec(memory_space=pl.ANY),
        ],
        out_specs=(
            pl.BlockSpec(memory_space=pltpu.VMEM),
            pl.BlockSpec(memory_space=pltpu.VMEM),
        ),
        scratch_shapes=[
            pltpu.VMEM((block_rows, slots, size, size), F32),
            pltpu.VMEM((block_rows, 2 * size, slots * size), BF16),
            pltpu.VMEM((block_rows, 2 * slots * size, size), BF16),
            pltpu.SMEM((block_rows * slots * tiles,), F32),
            pltpu.SMEM((block_rows * slots,), F32),
            pltpu.VMEM((tiles, columns, size), F32),
            pltpu.VMEM((tiles, columns, size), F32),
            pltpu.VMEM((2, tiles, columns, size), F32),
            pltpu.VMEM((2, group, columns, size), F32),
            pltpu.VMEM((2, block_rows, columns, size), F32),
            pltpu.VMEM((2, nbrs, columns, size), F32),
            pltpu.VMEM((columns, size), F32),
            pltpu.VMEM((tiles, columns // 4, size), F32),
            pltpu.VMEM((tiles, columns // 2, size), F32),
            pltpu.VMEM((block_rows, columns, size), F32),
            dma,
            dma((rows, block_rows)),
            dma((rows, block_rows)),
            dma((2, rows, block_rows)),
            dma((2, group)),
            dma((2, block_rows)),
            dma((2, nbrs)),
            dma((rows, nbrs)),
            dma((tiles,)),
            dma((tiles,)),
            dma((tiles,)),
            dma((group,)),
            dma((tiles,)),
            dma((nbrs,)),
            dma((block_rows,)),
        ],
        compiler_params=pltpu.CompilerParams(collective_id=0, has_side_effects=True),
    )(partner_ids, counts, start.T, blocks)
    return basis.T, ritz


def solution(mesh):
    rows, nbrs = mesh.shape["row"], mesh.shape["nbr"]

    def program(blocks, partner_ids, counts, start):
        block_rows = partner_ids.shape[0]
        size, columns = blocks.shape[2], start.shape[1]
        if rows * nbrs <= DIRECT_PEERS and block_rows <= nbrs and size == 128 and 4 * columns == size:
            return direct_body(rows, nbrs, blocks, partner_ids, counts, start)
        return body(blocks, partner_ids, counts, start)

    return jax.shard_map(
        program,
        mesh=mesh,
        in_specs=(
            P(("dom", "row"), "nbr", None, None),
            P(("dom", "row"), "nbr"),
            P(("dom", "row")),
            P(("dom", "row"), None),
        ),
        out_specs=(P(("dom", "row"), None), P("dom", None)),
        check_vma=False,
    )
```

```python
import functools

import jax
import jax.numpy as jnp
from jax import lax
from jax.experimental import pallas as pl
from jax.experimental.pallas import tpu as pltpu
from jax.sharding import PartitionSpec as P

ITERS = 2
DIRECT_PEERS = 16

HIGH = lax.Precision.HIGHEST
F32 = jnp.float32
BF16 = jnp.bfloat16


def orthonormal(image, gram, total):
    lower = jnp.linalg.cholesky(gram / total)
    return lax.linalg.triangular_solve(lower, image, left_side=False, lower=True, transpose_a=True)


def body(blocks, partner_ids, counts, start):
    block_rows, slots_here = partner_ids.shape
    block_size = blocks.shape[2]
    columns = start.shape[1]
    row_count = lax.axis_size("row")
    all_blocks = block_rows * row_count
    total = all_blocks * block_size
    first_row = lax.axis_index("row") * block_rows
    rows_here = first_row + jnp.arange(block_rows, dtype=jnp.int32)
    slot_index = lax.axis_index("nbr") * slots_here + jnp.arange(slots_here, dtype=jnp.int32)
    valid = slot_index[None, :] < counts[:, None]
    weight = jnp.where(valid, jnp.where(partner_ids == rows_here[:, None], 0.5, 1.0), 0.0).astype(
        jnp.float32
    )
    targets = jnp.concatenate([partner_ids.reshape(-1), rows_here])
    whole = lax.all_gather(start, "row", axis=0, tiled=True)
    cross = jnp.zeros((columns, columns), jnp.float32)
    prior = start
    for step in range(ITERS):
        tiles = whole.reshape(all_blocks, block_size, columns)
        far = tiles[partner_ids] * weight[:, :, None, None]
        near = lax.dynamic_slice_in_dim(tiles, first_row, block_rows, 0)
        direct = jnp.einsum("ipab,ipbk->iak", blocks, far, precision=HIGH)
        transposed = (
            jnp.einsum("ipab,iak->ipbk", blocks, near, precision=HIGH) * weight[:, :, None, None]
        )
        items = jnp.concatenate(
            [transposed.reshape(block_rows * slots_here, block_size, columns), direct], axis=0
        )
        placed = jnp.zeros((all_blocks, block_size, columns), jnp.float32).at[targets].add(items)
        summed = lax.psum_scatter(
            placed.reshape(total, columns), "row", scatter_dimension=0, tiled=True
        )
        image = lax.psum(summed, "nbr")
        gram, cross = lax.psum(
            (jnp.dot(image.T, image, precision=HIGH), jnp.dot(prior.T, image, precision=HIGH)),
            "row",
        )
        cross = cross / total
        prior = orthonormal(image, gram, total)
        if step + 1 < ITERS:
            whole = lax.all_gather(prior, "row", axis=0, tiled=True)
    return (prior, cross)


def split(x):
    high = x.astype(BF16)
    return high, (x - high.astype(F32)).astype(BF16)


def dot_nt(a, b):
    return lax.dot_general(a, b, (((1,), (1,)), ((), ())), precision=HIGH, preferred_element_type=F32)


def dot_nn(a, b, precision=HIGH):
    return lax.dot_general(
        a, b, (((1,), (0,)), ((), ())), precision=precision, preferred_element_type=F32
    )


def inverse_factor(gram_at, columns, lanes):
    row = lax.broadcasted_iota(jnp.int32, (columns, lanes), 0)
    lane = lax.broadcasted_iota(jnp.int32, (columns, lanes), 1)
    work = jnp.where(lane < columns, jnp.where(lane == row, 1.0, 0.0), gram_at)
    work = jnp.where(lane < 2 * columns, work, 0.0)
    for k in range(columns):
        pivot = work[k : k + 1, :]
        at = columns + k
        inverse = 1.0 / pivot[:, at : at + 1]
        factor = jnp.where(row[:, :1] > k, work[:, at : at + 1] * inverse, 0.0)
        work = work - factor * pivot
    diagonal = jnp.sum(jnp.where(lane == row + columns, work, 0.0), axis=1, keepdims=True)
    return (work * (1.0 / jnp.sqrt(diagonal)))[:, :columns]


def kernel(
    rows, nbrs, ids_ref, counts_ref, start_ref, blocks_ref, out_ref,
    held, straight, turned, sel, weight, begun, first_image, part, inbox, near_part, near_inbox, total_sum,
    grams, stats, images,
    blocks_sem, start_send, start_recv, relay_send, relay_recv, rs_send, rs_recv, near_send, near_recv, ag_send, ag_recv,
    gram_send, gram_recv, st_send, st_recv, im_send, im_recv,
):
    block_rows, slots = ids_ref.shape
    columns = start_ref.shape[0]
    size = blocks_ref.shape[2]
    tiles = block_rows * rows
    total = tiles * size
    group = rows * nbrs
    my_row, my_nbr = lax.axis_index("row"), lax.axis_index("nbr")
    me = my_row * nbrs + my_nbr
    owner = my_nbr < block_rows
    my_slot = lax.min(my_nbr, block_rows - 1)
    first_tile = my_row * block_rows
    my_tile = first_tile + my_slot
    whole = (begun, first_image)
    blank = jnp.zeros((columns, size), F32)
    half, quarter = columns // 2, columns // 4
    side = lax.rem(my_nbr, 2)
    partner = my_nbr + 1 - 2 * side

    def send(src, dst, send_sem, recv_sem, r, n):
        return pltpu.make_async_remote_copy(
            src_ref=src, dst_ref=dst, send_sem=send_sem, recv_sem=recv_sem,
            device_id={"row": r, "nbr": n}, device_id_type=pl.DeviceIdType.MESH,
        )

    barrier = pltpu.get_barrier_semaphore()
    for d in range(1, group):
        peer = lax.rem(me + d, group)
        pl.semaphore_signal(
            barrier, inc=1, device_id={"row": peer // nbrs, "nbr": lax.rem(peer, nbrs)},
            device_id_type=pl.DeviceIdType.MESH,
        )
    load = pltpu.make_async_copy(blocks_ref, held, blocks_sem)
    load.start()
    for i in range(block_rows):
        begun[first_tile + i] = start_ref[:, i * size : (i + 1) * size]
    for q in range(rows - 1):
        @pl.when(q < my_row)
        def _():
            for i in range(block_rows):
                begun[q * block_rows + i] = blank
                first_image[q * block_rows + i] = blank
    for i in range(block_rows):
        for p in range(slots):
            j = ids_ref[i, p]
            valid = my_nbr * slots + p < counts_ref[i]
            c = jnp.where(valid, jnp.where(j == first_tile + i, 0.5, 1.0), 0.0)
            weight[i * slots + p] = c
            for t in range(tiles):
                sel[(i * slots + p) * tiles + t] = jnp.where(j == t, c, 0.0)

    load.wait()
    span = slots * size
    for i in range(block_rows):
        for p in range(slots):
            block = held[i, p]
            high, low = split(block)
            straight[i, :size, p * size : (p + 1) * size] = high
            straight[i, size:, p * size : (p + 1) * size] = low
            high, low = split(block.T)
            turned[i, p * size : (p + 1) * size, :] = high
            turned[i, span + p * size : span + (p + 1) * size, :] = low

    def transposed(step):
        moved = []
        for i in range(block_rows):
            near = jnp.concatenate(split(whole[step][first_tile + i]), axis=0)
            out = dot_nn(jnp.concatenate([near, near], axis=1), straight[i], None)
            moved.append(out[:columns] + out[columns:])
        for t in range(tiles):
            summed = None
            for i in range(block_rows):
                for p in range(slots):
                    term = moved[i][:, p * size : (p + 1) * size] * sel[(i * slots + p) * tiles + t]
                    summed = term if summed is None else summed + term
            part[step, t] = summed

    def direct(step):
        for i in range(block_rows):
            far = []
            for p in range(slots):
                tile = whole[step][ids_ref[i, p]] * weight[i * slots + p]
                far.append(jnp.concatenate(split(tile), axis=0))
            out = dot_nn(jnp.concatenate(far + far, axis=1), turned[i], None)
            near_part[step, i] = out[:columns] + out[columns:]

    def half_at(ref, t, h):
        return ref.at[t, pl.ds(pl.multiple_of(h * half, half), half)]

    def start_copy(q, i):
        return send(
            start_ref.at[pl.ds(pl.multiple_of(side * half, half), half), pl.ds(i * size, size)],
            half_at(begun, first_tile + i, side),
            start_send.at[q, i], start_recv.at[my_row, i], q, my_nbr,
        )

    def start_wait(q, i):
        mine = half_at(begun, q * block_rows + i, side)
        send(mine, mine, start_send.at[q, i], start_recv.at[q, i], q, my_nbr).wait_recv()

    def relay(step, q, i):
        mine = half_at(whole[step], q * block_rows + i, side)
        return send(
            mine, mine, relay_send.at[step, q, i], relay_recv.at[step, q, i], my_row, partner
        )

    def relay_wait(step, q, i):
        other = half_at(whole[step], q * block_rows + i, 1 - side)
        send(
            other, other, relay_send.at[step, q, i], relay_recv.at[step, q, i], my_row, partner
        ).wait_recv()

    def each_later(act):
        for q in range(1, rows):
            @pl.when(q > my_row)
            def _():
                for i in range(block_rows):
                    act(q, i)

    def pass_on(step, wait):
        def act(q, i):
            wait(q, i)
            relay(step, q, i).start()

        each_later(act)
        each_later(lambda q, i: relay_wait(step, q, i))

    def sum_copy(step, r, n):
        return send(
            part.at[step, r * block_rows + n], inbox.at[step, me],
            rs_send.at[step, r, n], rs_recv.at[step, me], r, n,
        )

    def sum_wait(step, r, n):
        send(
            part.at[step, my_tile], inbox.at[step, r * nbrs + n],
            rs_send.at[step, 0, 0], rs_recv.at[step, r * nbrs + n], r, n,
        ).wait_recv()

    def each_sum(step, act):
        for r in range(rows):
            for n in range(block_rows):
                @pl.when(jnp.logical_and(r >= my_row, r * nbrs + n != me))
                def _():
                    act(sum_copy(step, r, n))

    def near_copy(step, i):
        return send(
            near_part.at[step, i], near_inbox.at[step, my_nbr],
            near_send.at[step, i], near_recv.at[step, my_nbr], my_row, i,
        )

    def near_wait(step, n):
        send(
            near_part.at[step, my_slot], near_inbox.at[step, n],
            near_send.at[step, 0], near_recv.at[step, n], my_row, n,
        ).wait_recv()

    def each_near(step, act):
        for i in range(block_rows):
            @pl.when(i != my_nbr)
            def _():
                act(near_copy(step, i))

    def gather_sums(step):
        total_sum[...] = part[step, my_tile] + near_part[step, my_slot]
        for q in range(rows - 1):
            @pl.when(q < my_row)
            def _():
                for n in range(nbrs):
                    sum_wait(step, q, n)
                summed = inbox[step, q * nbrs]
                for n in range(1, nbrs):
                    summed = summed + inbox[step, q * nbrs + n]
                total_sum[...] += summed
        for e in range(1, nbrs):
            n = lax.rem(my_nbr + e, nbrs)
            sum_wait(step, my_row, n)
            total_sum[...] += inbox[step, my_row * nbrs + n]
        for e in range(1, nbrs):
            n = lax.rem(my_nbr + e, nbrs)
            near_wait(step, n)
            total_sum[...] += near_inbox[step, n]
        return total_sum[...]

    def image_copy(r, n):
        return send(
            first_image.at[my_tile], first_image.at[my_tile],
            ag_send.at[r, n], ag_recv.at[my_tile], r, n,
        )

    def image_wait(t):
        send(
            first_image.at[t], first_image.at[t], ag_send.at[0, 0], ag_recv.at[t], my_row, my_nbr
        ).wait_recv()

    def near_images(act):
        for e in range(1, nbrs):
            act(image_copy(my_row, lax.rem(my_nbr + e, nbrs)))

    def far_images(act):
        for q in range(rows - 1):
            @pl.when(q < my_row)
            def _():
                for n in range(nbrs):
                    act(far_copy(q, n))

    def far_copy(q, n):
        piece = half_at(first_image, my_tile, n % 2)
        return send(piece, piece, ag_send.at[q, n], ag_recv.at[my_tile], q, n)

    def far_wait(q, i):
        t = q * block_rows + i
        mine = half_at(first_image, t, side)
        send(mine, mine, ag_send.at[0, 0], ag_recv.at[t], my_row, my_nbr).wait_recv()

    def gram_copy(t):
        return send(
            grams.at[my_tile], grams.at[my_tile],
            gram_send.at[t], gram_recv.at[my_tile], t // block_rows, t % block_rows,
        )

    def gram_wait(t):
        send(
            grams.at[t], grams.at[t], gram_send.at[t], gram_recv.at[t],
            t // block_rows, t % block_rows,
        ).wait_recv()

    def each_gram(act):
        for t in range(tiles):
            @pl.when(t != my_tile)
            def _():
                act(t)

    def stats_copy(kind, r, n):
        return send(
            stats.at[kind, my_tile], stats.at[kind, my_tile],
            st_send.at[kind, r, n], st_recv.at[kind, my_tile], r, n,
        )

    def stats_wait(kind):
        for t in range(tiles):
            @pl.when(jnp.logical_or(jnp.logical_not(owner), t != my_tile))
            def _():
                send(
                    stats.at[kind, t], stats.at[kind, t],
                    st_send.at[kind, 0, 0], st_recv.at[kind, t], my_row, my_nbr,
                ).wait_recv()

    def each_stats(kind, act):
        for k in range(rows):
            r = jnp.where(2 * my_row >= rows, k, rows - 1 - k)
            for e in range(nbrs):
                n = lax.rem(my_nbr + nbrs - 1 - e, nbrs)
                @pl.when(r * nbrs + n != me)
                def _():
                    act(stats_copy(kind, r, n))

    def pack(square):
        packed = square[:quarter]
        for g in range(1, 4):
            packed = packed + pltpu.roll(square[g * quarter : (g + 1) * quarter], g * columns, 1)
        return packed

    def unpack(parts):
        packed = parts[0]
        for t in range(1, tiles):
            packed = packed + parts[t]
        packed = packed / total
        return jnp.concatenate(
            [pltpu.roll(packed, size - g * columns, 1) if g else packed for g in range(4)], axis=0
        )

    def own_copy(e):
        return send(
            images.at[my_slot], images.at[my_slot],
            im_send.at[e - 1], im_recv.at[my_slot], my_row, lax.rem(my_nbr + e, nbrs),
        )

    def own_wait(i):
        send(
            images.at[i], images.at[i], im_send.at[0], im_recv.at[i], my_row, my_nbr
        ).wait_recv()

    def each_start(act):
        for q in range(rows - 1):
            @pl.when(q < my_row)
            def _():
                for i in range(block_rows):
                    act(start_copy(q, i))

    def begin(copy):
        copy.start()

    def end(copy):
        copy.wait_send()

    transposed(0)
    pl.semaphore_wait(barrier, group - 1)
    each_start(begin)
    each_sum(0, begin)
    pass_on(0, start_wait)
    direct(0)
    each_near(0, begin)

    @pl.when(owner)
    def _():
        tile = gather_sums(0)
        first_image[my_tile] = tile
        near_images(begin)
        far_images(begin)
        gram = dot_nt(tile, jnp.concatenate([tile, blank, blank, blank], axis=0))
        grams[my_tile] = pack(gram)
        each_gram(lambda t: gram_copy(t).start())

    for i in range(block_rows):
        @pl.when(i != my_nbr)
        def _():
            image_wait(first_tile + i)
    transposed(1)
    each_sum(1, begin)
    pass_on(1, far_wait)
    direct(1)
    each_near(1, begin)

    @pl.when(owner)
    def _():
        each_gram(gram_wait)
        gram = unpack(grams)
        first = inverse_factor(pltpu.roll(gram, columns, 1), columns, size)
        prior = dot_nn(first, first_image[my_tile])
        image = dot_nn(first, gather_sums(1))
        images[my_nbr] = image
        padded = jnp.concatenate([image, blank, blank, blank], axis=0)
        stats[0, my_tile] = pack(dot_nt(image, padded))
        each_stats(0, begin)
        for e in range(1, nbrs):
            own_copy(e).start()
        stats[1, my_tile] = pack(dot_nt(prior, padded))
        each_stats(1, begin)

    stats_wait(0)
    last = inverse_factor(pltpu.roll(unpack(stats.at[0]), columns, 1), columns, size)
    for i in range(block_rows):
        @pl.when(i != my_nbr)
        def _():
            own_wait(i)
    for i in range(block_rows):
        out_ref[:, i * size : (i + 1) * size] = dot_nn(last, images[i])
    stats_wait(1)
    out_ref[:, block_rows * size :] = unpack(stats.at[1])

    each_start(end)
    for step in range(ITERS):
        each_later(lambda q, i: relay(step, q, i).wait_send())
        each_sum(step, end)
        each_near(step, end)

    @pl.when(owner)
    def _():
        near_images(end)
        far_images(end)
        each_gram(lambda t: gram_copy(t).wait_send())
        each_stats(0, end)
        each_stats(1, end)
        for e in range(1, nbrs):
            own_copy(e).wait_send()


def part_outputs(joined_ref, basis_ref, ritz_ref):
    width = basis_ref.shape[1]
    basis_ref[...] = joined_ref[:, :width]
    ritz_ref[...] = joined_ref[:, width : width + ritz_ref.shape[1]]


def direct_body(rows, nbrs, blocks, partner_ids, counts, start):
    block_rows, slots = partner_ids.shape
    size = blocks.shape[2]
    columns = start.shape[1]
    tiles = block_rows * rows
    group = rows * nbrs
    dma = pltpu.SemaphoreType.DMA
    joined = pl.pallas_call(
        functools.partial(kernel, rows, nbrs),
        out_shape=jax.ShapeDtypeStruct((columns, (block_rows + 1) * size), F32),
        in_specs=[
            pl.BlockSpec(memory_space=pltpu.SMEM),
            pl.BlockSpec(memory_space=pltpu.SMEM),
            pl.BlockSpec(memory_space=pltpu.VMEM),
            pl.BlockSpec(memory_space=pltpu.HBM),
        ],
        out_specs=pl.BlockSpec(memory_space=pltpu.VMEM),
        scratch_shapes=[
            pltpu.VMEM((block_rows, slots, size, size), F32),
            pltpu.VMEM((block_rows, 2 * size, slots * size), BF16),
            pltpu.VMEM((block_rows, 2 * slots * size, size), BF16),
            pltpu.SMEM((block_rows * slots * tiles,), F32),
            pltpu.SMEM((block_rows * slots,), F32),
            pltpu.VMEM((tiles, columns, size), F32),
            pltpu.VMEM((tiles, columns, size), F32),
            pltpu.VMEM((2, tiles, columns, size), F32),
            pltpu.VMEM((2, group, columns, size), F32),
            pltpu.VMEM((2, block_rows, columns, size), F32),
            pltpu.VMEM((2, nbrs, columns, size), F32),
            pltpu.VMEM((columns, size), F32),
            pltpu.VMEM((tiles, columns // 4, size), F32),
            pltpu.VMEM((2, tiles, columns // 4, size), F32),
            pltpu.VMEM((block_rows, columns, size), F32),
            dma,
            dma((rows, block_rows)),
            dma((rows, block_rows)),
            dma((2, rows, block_rows)),
            dma((2, rows, block_rows)),
            dma((2, rows, block_rows)),
            dma((2, group)),
            dma((2, block_rows)),
            dma((2, nbrs)),
            dma((rows, nbrs)),
            dma((tiles,)),
            dma((tiles,)),
            dma((tiles,)),
            dma((2, rows, nbrs)),
            dma((2, tiles)),
            dma((nbrs,)),
            dma((block_rows,)),
        ],
        compiler_params=pltpu.CompilerParams(collective_id=0, has_side_effects=True),
    )(partner_ids, counts, start.T, blocks)
    basis, ritz = pl.pallas_call(
        part_outputs,
        out_shape=(
            jax.ShapeDtypeStruct((columns, block_rows * size), F32),
            jax.ShapeDtypeStruct((columns, columns), F32),
        ),
        in_specs=[pl.BlockSpec(memory_space=pltpu.VMEM)],
        out_specs=(
            pl.BlockSpec(memory_space=pltpu.VMEM),
            pl.BlockSpec(memory_space=pltpu.VMEM),
        ),
    )(joined)
    return basis.T, ritz


def solution(mesh):
    rows, nbrs = mesh.shape["row"], mesh.shape["nbr"]

    def program(blocks, partner_ids, counts, start):
        block_rows = partner_ids.shape[0]
        size, columns = blocks.shape[2], start.shape[1]
        if rows * nbrs <= DIRECT_PEERS and block_rows <= nbrs and nbrs % 2 == 0 and size == 128 and 4 * columns == size:
            return direct_body(rows, nbrs, blocks, partner_ids, counts, start)
        return body(blocks, partner_ids, counts, start)

    return jax.shard_map(
        program,
        mesh=mesh,
        in_specs=(
            P(("dom", "row"), "nbr", None, None),
            P(("dom", "row"), "nbr"),
            P(("dom", "row")),
            P(("dom", "row"), None),
        ),
        out_specs=(P(("dom", "row"), None), P("dom", None)),
        check_vma=False,
    )
```

```python
import functools

import jax
import jax.numpy as jnp
from jax import lax
from jax.experimental import pallas as pl
from jax.experimental.pallas import tpu as pltpu
from jax.sharding import PartitionSpec as P

ITERS = 2
DIRECT_PEERS = 16

HIGH = lax.Precision.HIGHEST
F32 = jnp.float32
BF16 = jnp.bfloat16


def orthonormal(image, gram, total):
    lower = jnp.linalg.cholesky(gram / total)
    return lax.linalg.triangular_solve(lower, image, left_side=False, lower=True, transpose_a=True)


def body(blocks, partner_ids, counts, start):
    block_rows, slots_here = partner_ids.shape
    block_size = blocks.shape[2]
    columns = start.shape[1]
    row_count = lax.axis_size("row")
    all_blocks = block_rows * row_count
    total = all_blocks * block_size
    first_row = lax.axis_index("row") * block_rows
    rows_here = first_row + jnp.arange(block_rows, dtype=jnp.int32)
    slot_index = lax.axis_index("nbr") * slots_here + jnp.arange(slots_here, dtype=jnp.int32)
    valid = slot_index[None, :] < counts[:, None]
    weight = jnp.where(valid, jnp.where(partner_ids == rows_here[:, None], 0.5, 1.0), 0.0).astype(
        jnp.float32
    )
    targets = jnp.concatenate([partner_ids.reshape(-1), rows_here])
    whole = lax.all_gather(start, "row", axis=0, tiled=True)
    cross = jnp.zeros((columns, columns), jnp.float32)
    prior = start
    for step in range(ITERS):
        tiles = whole.reshape(all_blocks, block_size, columns)
        far = tiles[partner_ids] * weight[:, :, None, None]
        near = lax.dynamic_slice_in_dim(tiles, first_row, block_rows, 0)
        direct = jnp.einsum("ipab,ipbk->iak", blocks, far, precision=HIGH)
        transposed = (
            jnp.einsum("ipab,iak->ipbk", blocks, near, precision=HIGH) * weight[:, :, None, None]
        )
        items = jnp.concatenate(
            [transposed.reshape(block_rows * slots_here, block_size, columns), direct], axis=0
        )
        placed = jnp.zeros((all_blocks, block_size, columns), jnp.float32).at[targets].add(items)
        summed = lax.psum_scatter(
            placed.reshape(total, columns), "row", scatter_dimension=0, tiled=True
        )
        image = lax.psum(summed, "nbr")
        gram, cross = lax.psum(
            (jnp.dot(image.T, image, precision=HIGH), jnp.dot(prior.T, image, precision=HIGH)),
            "row",
        )
        cross = cross / total
        prior = orthonormal(image, gram, total)
        if step + 1 < ITERS:
            whole = lax.all_gather(prior, "row", axis=0, tiled=True)
    return (prior, cross)


def split(x):
    high = x.astype(BF16)
    return high, (x - high.astype(F32)).astype(BF16)


def dot_nt(a, b):
    return lax.dot_general(a, b, (((1,), (1,)), ((), ())), precision=HIGH, preferred_element_type=F32)


def dot_nn(a, b, precision=HIGH):
    return lax.dot_general(
        a, b, (((1,), (0,)), ((), ())), precision=precision, preferred_element_type=F32
    )


def inverse_factor(gram_at, columns, lanes):
    row = lax.broadcasted_iota(jnp.int32, (columns, lanes), 0)
    lane = lax.broadcasted_iota(jnp.int32, (columns, lanes), 1)
    work = jnp.where(lane < columns, jnp.where(lane == row, 1.0, 0.0), gram_at)
    work = jnp.where(lane < 2 * columns, work, 0.0)
    for k in range(columns):
        pivot = work[k : k + 1, :]
        at = columns + k
        inverse = 1.0 / pivot[:, at : at + 1]
        factor = jnp.where(row[:, :1] > k, work[:, at : at + 1] * inverse, 0.0)
        work = work - factor * pivot
    diagonal = jnp.sum(jnp.where(lane == row + columns, work, 0.0), axis=1, keepdims=True)
    return (work * (1.0 / jnp.sqrt(diagonal)))[:, :columns]


def kernel(
    rows, nbrs, ids_ref, counts_ref, start_ref, blocks_ref, out_ref,
    held, straight, turned, sel, weight, begun, first_image, part, pair_in, pair_sum, inbox, near_part, near_inbox, total_sum,
    grams, stats, images,
    blocks_sem, start_send, start_recv, relay_send, relay_recv, pair_send, pair_recv, rs_send, rs_recv, near_send, near_recv, ag_send, ag_recv,
    gram_send, gram_recv, st_send, st_recv, im_send, im_recv,
):
    block_rows, slots = ids_ref.shape
    columns = start_ref.shape[0]
    size = blocks_ref.shape[2]
    tiles = block_rows * rows
    total = tiles * size
    group = rows * nbrs
    my_row, my_nbr = lax.axis_index("row"), lax.axis_index("nbr")
    me = my_row * nbrs + my_nbr
    owner = my_nbr < block_rows
    my_slot = lax.min(my_nbr, block_rows - 1)
    first_tile = my_row * block_rows
    my_tile = first_tile + my_slot
    whole = (begun, first_image)
    blank = jnp.zeros((columns, size), F32)
    half, quarter = columns // 2, columns // 4
    side = lax.rem(my_nbr, 2)
    partner = my_nbr + 1 - 2 * side

    def send(src, dst, send_sem, recv_sem, r, n):
        return pltpu.make_async_remote_copy(
            src_ref=src, dst_ref=dst, send_sem=send_sem, recv_sem=recv_sem,
            device_id={"row": r, "nbr": n}, device_id_type=pl.DeviceIdType.MESH,
        )

    barrier = pltpu.get_barrier_semaphore()
    for d in range(1, group):
        peer = lax.rem(me + d, group)
        pl.semaphore_signal(
            barrier, inc=1, device_id={"row": peer // nbrs, "nbr": lax.rem(peer, nbrs)},
            device_id_type=pl.DeviceIdType.MESH,
        )
    load = pltpu.make_async_copy(blocks_ref, held, blocks_sem)
    load.start()
    for i in range(block_rows):
        begun[first_tile + i] = start_ref[:, i * size : (i + 1) * size]
    for q in range(rows - 1):
        @pl.when(q < my_row)
        def _():
            for i in range(block_rows):
                begun[q * block_rows + i] = blank
                first_image[q * block_rows + i] = blank
    for i in range(block_rows):
        for p in range(slots):
            j = ids_ref[i, p]
            valid = my_nbr * slots + p < counts_ref[i]
            c = jnp.where(valid, jnp.where(j == first_tile + i, 0.5, 1.0), 0.0)
            weight[i * slots + p] = c
            for t in range(tiles):
                sel[(i * slots + p) * tiles + t] = jnp.where(j == t, c, 0.0)

    load.wait()
    span = slots * size
    for i in range(block_rows):
        for p in range(slots):
            block = held[i, p]
            high, low = split(block)
            straight[i, :size, p * size : (p + 1) * size] = high
            straight[i, size:, p * size : (p + 1) * size] = low
            high, low = split(block.T)
            turned[i, p * size : (p + 1) * size, :] = high
            turned[i, span + p * size : span + (p + 1) * size, :] = low

    def transposed(step):
        moved = []
        for i in range(block_rows):
            near = jnp.concatenate(split(whole[step][first_tile + i]), axis=0)
            out = dot_nn(jnp.concatenate([near, near], axis=1), straight[i], None)
            moved.append(out[:columns] + out[columns:])
        for t in range(tiles):
            summed = None
            for i in range(block_rows):
                for p in range(slots):
                    term = moved[i][:, p * size : (p + 1) * size] * sel[(i * slots + p) * tiles + t]
                    summed = term if summed is None else summed + term
            part[step, t] = summed

    def direct(step):
        for i in range(block_rows):
            far = []
            for p in range(slots):
                tile = whole[step][ids_ref[i, p]] * weight[i * slots + p]
                far.append(jnp.concatenate(split(tile), axis=0))
            out = dot_nn(jnp.concatenate(far + far, axis=1), turned[i], None)
            near_part[step, i] = out[:columns] + out[columns:]

    def half_at(ref, t, h):
        return ref.at[t, pl.ds(pl.multiple_of(h * half, half), half)]

    def start_copy(q, i):
        return send(
            start_ref.at[pl.ds(pl.multiple_of(side * half, half), half), pl.ds(i * size, size)],
            half_at(begun, first_tile + i, side),
            start_send.at[q, i], start_recv.at[my_row, i], q, my_nbr,
        )

    def start_wait(q, i):
        mine = half_at(begun, q * block_rows + i, side)
        send(mine, mine, start_send.at[q, i], start_recv.at[q, i], q, my_nbr).wait_recv()

    def relay(step, q, i):
        mine = half_at(whole[step], q * block_rows + i, side)
        return send(
            mine, mine, relay_send.at[step, q, i], relay_recv.at[step, q, i], my_row, partner
        )

    def relay_wait(step, q, i):
        other = half_at(whole[step], q * block_rows + i, 1 - side)
        send(
            other, other, relay_send.at[step, q, i], relay_recv.at[step, q, i], my_row, partner
        ).wait_recv()

    def each_later(act):
        for q in range(1, rows):
            @pl.when(q > my_row)
            def _():
                for i in range(block_rows):
                    act(q, i)

    def pass_on(step, wait):
        def act(q, i):
            wait(q, i)
            relay(step, q, i).start()

        each_later(act)
        each_later(lambda q, i: relay_wait(step, q, i))

    def sum_copy(step, r, n):
        return send(
            pair_sum.at[step, r * block_rows + n], inbox.at[step, me],
            rs_send.at[step, r, n], rs_recv.at[step, me], r, n,
        )

    def sum_wait(step, r, n):
        send(
            pair_sum.at[step, my_tile], inbox.at[step, r * nbrs + n],
            rs_send.at[step, 0, 0], rs_recv.at[step, r * nbrs + n], r, n,
        ).wait_recv()

    def pair_copy(step, r):
        here = pl.ds(r * block_rows, block_rows)
        theirs = pl.ds(pl.multiple_of((1 - side) * half, half), half)
        return send(
            part.at[step, here, theirs], pair_in.at[step, here],
            pair_send.at[step, r], pair_recv.at[step, r], my_row, partner,
        )

    def each_pair(step, act):
        for r in reversed(range(rows)):
            @pl.when(r >= my_row)
            def _():
                act(r)

    def send_sums(step):
        each_pair(step, lambda r: pair_copy(step, r).start())

        def finish(r):
            pair_copy(step, r).wait_recv()
            for t in range(r * block_rows, (r + 1) * block_rows):
                own = part[step, t, pl.ds(pl.multiple_of(side * half, half), half)]
                pair_sum[step, t] = own + pair_in[step, t]

        each_pair(step, finish)
        each_sum(step, begin)

    def each_sum(step, act):
        for r in reversed(range(rows)):
            for n in range(block_rows):
                @pl.when(jnp.logical_and(r >= my_row, r * nbrs + n != me))
                def _():
                    act(sum_copy(step, r, n))

    def near_copy(step, i):
        return send(
            near_part.at[step, i], near_inbox.at[step, my_nbr],
            near_send.at[step, i], near_recv.at[step, my_nbr], my_row, i,
        )

    def near_wait(step, n):
        send(
            near_part.at[step, my_slot], near_inbox.at[step, n],
            near_send.at[step, 0], near_recv.at[step, n], my_row, n,
        ).wait_recv()

    def each_near(step, act):
        for i in range(block_rows):
            @pl.when(i != my_nbr)
            def _():
                act(near_copy(step, i))

    def gather_sums(step):
        total_sum[...] = near_part[step, my_slot]
        inbox[step, me] = pair_sum[step, my_tile]

        def add(q):
            for h in range(2):
                summed = inbox[step, q * nbrs + h]
                for n in range(h + 2, nbrs, 2):
                    summed = summed + inbox[step, q * nbrs + n]
                total_sum[h * half : (h + 1) * half, :] += summed

        for e in range(1, nbrs):
            sum_wait(step, my_row, lax.rem(my_nbr + e, nbrs))
        add(my_row)
        for q in reversed(range(rows - 1)):
            @pl.when(q < my_row)
            def _():
                for n in range(nbrs):
                    sum_wait(step, q, n)
                add(q)
        for e in range(1, nbrs):
            n = lax.rem(my_nbr + e, nbrs)
            near_wait(step, n)
            total_sum[...] += near_inbox[step, n]
        return total_sum[...]

    def image_copy(r, n):
        return send(
            first_image.at[my_tile], first_image.at[my_tile],
            ag_send.at[r, n], ag_recv.at[my_tile], r, n,
        )

    def image_wait(t):
        send(
            first_image.at[t], first_image.at[t], ag_send.at[0, 0], ag_recv.at[t], my_row, my_nbr
        ).wait_recv()

    def near_images(act):
        for e in range(1, nbrs):
            act(image_copy(my_row, lax.rem(my_nbr + e, nbrs)))

    def far_images(act):
        for q in range(rows - 1):
            @pl.when(q < my_row)
            def _():
                for n in range(nbrs):
                    act(far_copy(q, n))

    def far_copy(q, n):
        piece = half_at(first_image, my_tile, n % 2)
        return send(piece, piece, ag_send.at[q, n], ag_recv.at[my_tile], q, n)

    def far_wait(q, i):
        t = q * block_rows + i
        mine = half_at(first_image, t, side)
        send(mine, mine, ag_send.at[0, 0], ag_recv.at[t], my_row, my_nbr).wait_recv()

    def gram_copy(t):
        return send(
            grams.at[my_tile], grams.at[my_tile],
            gram_send.at[t], gram_recv.at[my_tile], t // block_rows, t % block_rows,
        )

    def gram_wait(t):
        send(
            grams.at[t], grams.at[t], gram_send.at[t], gram_recv.at[t],
            t // block_rows, t % block_rows,
        ).wait_recv()

    def each_gram(act):
        for t in range(tiles):
            @pl.when(t != my_tile)
            def _():
                act(t)

    def stats_copy(kind, r, n):
        return send(
            stats.at[kind, my_tile], stats.at[kind, my_tile],
            st_send.at[kind, r, n], st_recv.at[kind, my_tile], r, n,
        )

    def stats_wait(kind):
        for t in range(tiles):
            @pl.when(jnp.logical_or(jnp.logical_not(owner), t != my_tile))
            def _():
                send(
                    stats.at[kind, t], stats.at[kind, t],
                    st_send.at[kind, 0, 0], st_recv.at[kind, t], my_row, my_nbr,
                ).wait_recv()

    def each_stats(kind, act):
        for k in range(rows):
            r = jnp.where(2 * my_row >= rows, k, rows - 1 - k)
            for e in range(nbrs):
                n = lax.rem(my_nbr + nbrs - 1 - e, nbrs)
                @pl.when(r * nbrs + n != me)
                def _():
                    act(stats_copy(kind, r, n))

    def pack(square):
        packed = square[:quarter]
        for g in range(1, 4):
            packed = packed + pltpu.roll(square[g * quarter : (g + 1) * quarter], g * columns, 1)
        return packed

    def unpack(parts):
        packed = parts[0]
        for t in range(1, tiles):
            packed = packed + parts[t]
        packed = packed / total
        return jnp.concatenate(
            [pltpu.roll(packed, size - g * columns, 1) if g else packed for g in range(4)], axis=0
        )

    def own_copy(e):
        return send(
            images.at[my_slot], images.at[my_slot],
            im_send.at[e - 1], im_recv.at[my_slot], my_row, lax.rem(my_nbr + e, nbrs),
        )

    def own_wait(i):
        send(
            images.at[i], images.at[i], im_send.at[0], im_recv.at[i], my_row, my_nbr
        ).wait_recv()

    def each_start(act):
        for q in range(rows - 1):
            @pl.when(q < my_row)
            def _():
                for i in range(block_rows):
                    act(start_copy(q, i))

    def begin(copy):
        copy.start()

    def end(copy):
        copy.wait_send()

    transposed(0)
    pl.semaphore_wait(barrier, group - 1)
    each_start(begin)
    send_sums(0)
    pass_on(0, start_wait)
    direct(0)
    each_near(0, begin)

    @pl.when(owner)
    def _():
        tile = gather_sums(0)
        first_image[my_tile] = tile
        near_images(begin)
        far_images(begin)
        gram = dot_nt(tile, jnp.concatenate([tile, blank, blank, blank], axis=0))
        grams[my_tile] = pack(gram)
        each_gram(lambda t: gram_copy(t).start())

    for i in range(block_rows):
        @pl.when(i != my_nbr)
        def _():
            image_wait(first_tile + i)
    transposed(1)
    send_sums(1)
    pass_on(1, far_wait)
    direct(1)
    each_near(1, begin)

    @pl.when(owner)
    def _():
        each_gram(gram_wait)
        gram = unpack(grams)
        first = inverse_factor(pltpu.roll(gram, columns, 1), columns, size)
        prior = dot_nn(first, first_image[my_tile])
        image = dot_nn(first, gather_sums(1))
        images[my_nbr] = image
        padded = jnp.concatenate([image, blank, blank, blank], axis=0)
        stats[0, my_tile] = pack(dot_nt(image, padded))
        each_stats(0, begin)
        for e in range(1, nbrs):
            own_copy(e).start()
        stats[1, my_tile] = pack(dot_nt(prior, padded))
        each_stats(1, begin)

    stats_wait(0)
    last = inverse_factor(pltpu.roll(unpack(stats.at[0]), columns, 1), columns, size)
    for i in range(block_rows):
        @pl.when(i != my_nbr)
        def _():
            own_wait(i)
    for i in range(block_rows):
        out_ref[:, i * size : (i + 1) * size] = dot_nn(last, images[i])
    stats_wait(1)
    out_ref[:, block_rows * size :] = unpack(stats.at[1])

    each_start(end)
    for step in range(ITERS):
        each_later(lambda q, i: relay(step, q, i).wait_send())
        each_pair(step, lambda r: pair_copy(step, r).wait_send())
        each_sum(step, end)
        each_near(step, end)

    @pl.when(owner)
    def _():
        near_images(end)
        far_images(end)
        each_gram(lambda t: gram_copy(t).wait_send())
        each_stats(0, end)
        each_stats(1, end)
        for e in range(1, nbrs):
            own_copy(e).wait_send()


def part_outputs(joined_ref, basis_ref, ritz_ref):
    width = basis_ref.shape[1]
    basis_ref[...] = joined_ref[:, :width]
    ritz_ref[...] = joined_ref[:, width : width + ritz_ref.shape[1]]


def direct_body(rows, nbrs, blocks, partner_ids, counts, start):
    block_rows, slots = partner_ids.shape
    size = blocks.shape[2]
    columns = start.shape[1]
    tiles = block_rows * rows
    group = rows * nbrs
    dma = pltpu.SemaphoreType.DMA
    joined = pl.pallas_call(
        functools.partial(kernel, rows, nbrs),
        out_shape=jax.ShapeDtypeStruct((columns, (block_rows + 1) * size), F32),
        in_specs=[
            pl.BlockSpec(memory_space=pltpu.SMEM),
            pl.BlockSpec(memory_space=pltpu.SMEM),
            pl.BlockSpec(memory_space=pltpu.VMEM),
            pl.BlockSpec(memory_space=pltpu.HBM),
        ],
        out_specs=pl.BlockSpec(memory_space=pltpu.VMEM),
        scratch_shapes=[
            pltpu.VMEM((block_rows, slots, size, size), F32),
            pltpu.VMEM((block_rows, 2 * size, slots * size), BF16),
            pltpu.VMEM((block_rows, 2 * slots * size, size), BF16),
            pltpu.SMEM((block_rows * slots * tiles,), F32),
            pltpu.SMEM((block_rows * slots,), F32),
            pltpu.VMEM((tiles, columns, size), F32),
            pltpu.VMEM((tiles, columns, size), F32),
            pltpu.VMEM((2, tiles, columns, size), F32),
            pltpu.VMEM((2, tiles, columns // 2, size), F32),
            pltpu.VMEM((2, tiles, columns // 2, size), F32),
            pltpu.VMEM((2, group, columns // 2, size), F32),
            pltpu.VMEM((2, block_rows, columns, size), F32),
            pltpu.VMEM((2, nbrs, columns, size), F32),
            pltpu.VMEM((columns, size), F32),
            pltpu.VMEM((tiles, columns // 4, size), F32),
            pltpu.VMEM((2, tiles, columns // 4, size), F32),
            pltpu.VMEM((block_rows, columns, size), F32),
            dma,
            dma((rows, block_rows)),
            dma((rows, block_rows)),
            dma((2, rows, block_rows)),
            dma((2, rows, block_rows)),
            dma((2, rows)),
            dma((2, rows)),
            dma((2, rows, block_rows)),
            dma((2, group)),
            dma((2, block_rows)),
            dma((2, nbrs)),
            dma((rows, nbrs)),
            dma((tiles,)),
            dma((tiles,)),
            dma((tiles,)),
            dma((2, rows, nbrs)),
            dma((2, tiles)),
            dma((nbrs,)),
            dma((block_rows,)),
        ],
        compiler_params=pltpu.CompilerParams(collective_id=0, has_side_effects=True),
    )(partner_ids, counts, start.T, blocks)
    basis, ritz = pl.pallas_call(
        part_outputs,
        out_shape=(
            jax.ShapeDtypeStruct((columns, block_rows * size), F32),
            jax.ShapeDtypeStruct((columns, columns), F32),
        ),
        in_specs=[pl.BlockSpec(memory_space=pltpu.VMEM)],
        out_specs=(
            pl.BlockSpec(memory_space=pltpu.VMEM),
            pl.BlockSpec(memory_space=pltpu.VMEM),
        ),
    )(joined)
    return basis.T, ritz


def solution(mesh):
    rows, nbrs = mesh.shape["row"], mesh.shape["nbr"]

    def program(blocks, partner_ids, counts, start):
        block_rows = partner_ids.shape[0]
        size, columns = blocks.shape[2], start.shape[1]
        if rows * nbrs <= DIRECT_PEERS and block_rows <= nbrs and nbrs % 2 == 0 and size == 128 and 4 * columns == size:
            return direct_body(rows, nbrs, blocks, partner_ids, counts, start)
        return body(blocks, partner_ids, counts, start)

    return jax.shard_map(
        program,
        mesh=mesh,
        in_specs=(
            P(("dom", "row"), "nbr", None, None),
            P(("dom", "row"), "nbr"),
            P(("dom", "row")),
            P(("dom", "row"), None),
        ),
        out_specs=(P(("dom", "row"), None), P("dom", None)),
        check_vma=False,
    )
```
